32 devices in a mesh: grp: 4 (over z), wide: 8 (over y, x, core).
Axes of the slice: x: 2, y: 2, z: 4, core: 2. Of those that a mesh axis runs over, the one named last changes fastest.
Arguments:
- a_vals: bfloat16 [1024, 7, 128, 128], P(('grp', 'wide')), may hold values from -0.5 to 0.5
- a_cols: int32 [1024, 7], P(('grp', 'wide')), may hold values from 0 to 1023, as said below
- p_vals: bfloat16 [1024, 128, 128], P(('grp', 'wide')), may hold values from -1.75 to 1.75
- tile_slot: int32 [1024, 7], P(('grp', 'wide')), may hold values from 0 to 2047, as said below
Outputs:
- coarse: float32 [2048, 128, 128], P(('grp', 'wide'))
The draws below stay inside these ranges and needn't reach their ends.
Inputs may be any that keep to these rules, and one draw needn't show every extreme that they name: `a_cols`: entry 0 of fine block row i is i itself; every entry j satisfies (j // 32) % 8 = (i // 32) % 8. `tile_slot`: the 7 entries of a fine block row name different slots of one coarse block row, all below the same multiple of 8; the slot's device s // 64 has the same grp index (s // 64) // 8 as the row's device (i // 32) // 8. The fine block rows of one device send to one device at most 8 rows; in every draw some device receives exactly 8 rows from every device of its grp index.
All inputs are finite; a program needn't handle non-finite values.
Results may differ from the reference program's by a relative error of at most 0.005.
Values may be sent and summed in bfloat16 or wider, within the bound.
No kernel may reach another device: no remote copies, remote signals or barrier semaphores. Data moves between devices by JAX's collectives and lax.ppermute only.
A program may use at most 192 MiB of HBM per device.

```python
import jax
import jax.numpy as jnp
from jax import lax

B = 128
K = 7
KC = 8
NB_DEV = 32
CR_DEV = 8
OWNERS = 8
GROUPS = 4
RMOST = 8
FINE = 1024
SLOTS = 2048


def draw_a_cols(key, part):
    first_key, second_key = jax.random.split(key, 2)
    row_ids = jnp.arange(FINE, dtype=jnp.int32)
    wide_of = row_ids // NB_DEV % OWNERS
    plane_pick = jax.random.randint(first_key, (FINE, K), 0, GROUPS)
    row_pick = jax.random.randint(second_key, (FINE, K), 0, NB_DEV)
    columns = (plane_pick * OWNERS + wide_of[:, None]) * NB_DEV + row_pick
    columns = jnp.where(jnp.arange(K)[None, :] == 0, row_ids[:, None], columns)
    return columns.astype(jnp.int32)


def draw_tile_slot(key, part):
    subkeys = jax.random.split(key, 5)
    device_count = FINE // NB_DEV
    device = jnp.arange(device_count, dtype=jnp.int32)
    plane = device // OWNERS
    heavy_owner = jax.random.randint(subkeys[0], (GROUPS,), 0, OWNERS)[plane]
    scores = jax.random.randint(subkeys[1], (device_count, OWNERS - 1), 0, 1 << 20) * (OWNERS - 1) + jnp.arange(OWNERS - 1)
    others = jnp.argsort(scores, axis=1).astype(jnp.int32)
    row_index = jnp.arange(NB_DEV, dtype=jnp.int32)
    cycle_pos = jnp.maximum(row_index - RMOST, 0) % (OWNERS - 1)
    other_owner = (heavy_owner[:, None] + 1 + others[:, cycle_pos]) % OWNERS
    base_owner = jnp.where(row_index[None, :] < RMOST, heavy_owner[:, None], other_owner)
    row_scores = jax.random.randint(subkeys[2], (device_count, NB_DEV), 0, 1 << 20) * NB_DEV + row_index
    row_order = jnp.argsort(row_scores, axis=1)
    owner_of = jnp.take_along_axis(base_owner, row_order, axis=1).reshape(FINE)
    coarse_row = jax.random.randint(subkeys[3], (FINE,), 0, CR_DEV)
    column_scores = jax.random.randint(subkeys[4], (FINE, KC), 0, 1 << 20) * KC + jnp.arange(KC)
    column = jnp.argsort(column_scores, axis=1)[:, :K]
    plane_row = jnp.repeat(plane, NB_DEV)
    slot_ids = ((plane_row * OWNERS + owner_of) * CR_DEV + coarse_row)[:, None] * KC + column
    return slot_ids.astype(jnp.int32)


def block_scale(own_key, dims, pieces, smallest, largest):
    gain = 1.0
    for axis_at, blocks in pieces:
        steps = jax.random.uniform(jax.random.fold_in(jax.random.fold_in(own_key, 6), axis_at), (blocks,), jnp.float32, smallest / len(pieces), largest / len(pieces))
        gain = gain * jnp.repeat(jnp.exp(steps), dims[axis_at] // blocks).reshape((-1,) + (1,) * (len(dims) - 1 - axis_at))
    return gain


def bell_draw(own_key, extent, spread, bound, cuts=(), kind=jnp.bfloat16):
    level = block_scale(own_key, extent, cuts, -0.22, 0.18) if cuts else 1.0
    result = jax.random.normal(own_key, extent, jnp.float32) * spread * level
    return jnp.minimum(jnp.maximum(result, -bound), bound).astype(kind)


def setup_inputs(seed: int = 0) -> dict:
    splits = jax.random.split(jax.random.key(seed), 5)
    a_vals = bell_draw(splits[0], (FINE, K, B, B), B ** -0.5, 0.5, ((0, 32),))
    a_cols = draw_a_cols(jax.random.fold_in(splits[4], 71), 0)
    p_vals = bell_draw(splits[2], (FINE, B, B), 0.3, 1.75, ((0, 32),))
    tile_slot = draw_tile_slot(jax.random.fold_in(splits[4], 71), 0)
    return {"a_vals": a_vals, "a_cols": a_cols, "p_vals": p_vals, "tile_slot": tile_slot}


def reference(a_vals, a_cols, p_vals, tile_slot):
    fine_count = a_vals.shape[0]
    block_count = fine_count // NB_DEV

    def advance(coarse, block_index):
        first_row = block_index * NB_DEV
        a_block = lax.dynamic_slice_in_dim(a_vals, first_row, NB_DEV, 0)
        columns = lax.dynamic_slice_in_dim(a_cols, first_row, NB_DEV, 0)
        slot_ids = lax.dynamic_slice_in_dim(tile_slot, first_row, NB_DEV, 0)
        own_rows = lax.dynamic_slice_in_dim(p_vals, first_row, NB_DEV, 0)
        neighbours = p_vals[columns]
        product = jnp.einsum("rkab,rkbc->rkac", a_block.astype(jnp.float32), neighbours.astype(jnp.float32))
        product = lax.optimization_barrier(product.astype(jnp.bfloat16))
        tile_terms = jnp.einsum("rab,rkac->rkbc", own_rows.astype(jnp.float32), product.astype(jnp.float32))
        tile_terms = lax.optimization_barrier(tile_terms.astype(jnp.bfloat16)).astype(jnp.float32)
        coarse = coarse.at[slot_ids.reshape(-1)].add(tile_terms.reshape(-1, B, B))
        return coarse, None

    start_value = jnp.zeros((SLOTS, B, B), jnp.float32)
    coarse, unused = lax.scan(advance, start_value, jnp.arange(block_count, dtype=jnp.int32))
    return coarse
```

```python
import functools

import jax
import jax.numpy as jnp
from jax import lax
from jax.experimental import pallas as pl
from jax.experimental.pallas import tpu as pltpu
from jax.sharding import PartitionSpec as P

ROW_BLOCK = 4
VMEM_BYTES = 60 * 2**20


def flip(size, bit):
    return [(i, i ^ bit) for i in range(size)]


def transpose_kernel(p_ref, *chunk_refs):
    for row in range(p_ref.shape[0]):
        turned = p_ref[row].T
        first = 0
        for chunk in chunk_refs:
            rows = chunk.shape[1]
            chunk[row] = turned[first : first + rows]
            first += rows


def transposed_chunks(p_vals, heights):
    rows, side, _ = p_vals.shape
    block = 8
    return pl.pallas_call(
        transpose_kernel,
        grid=(rows // block,),
        in_specs=[pl.BlockSpec((block, side, side), lambda i: (i, 0, 0))],
        out_specs=[pl.BlockSpec((block, h, side), lambda i: (i, 0, 0)) for h in heights],
        out_shape=[jax.ShapeDtypeStruct((rows, h, side), p_vals.dtype) for h in heights],
        name="turn",
    )(p_vals)


def partial_kernel(pos_ref, dst_ref, a_ref, p_ref, *refs):
    planes = len(refs) - 4
    parts = refs[:planes]
    send_ref, keep_ref, near, total = refs[planes:]
    step = pl.program_id(0)
    row_block, per_row = a_ref.shape[0], a_ref.shape[1]
    height = near.shape[1]

    @pl.when(step == 0)
    def _():
        rows = parts[0].shape[0]
        for plane, part in enumerate(parts):
            near[plane * rows : (plane + 1) * rows] = part[...]
        total[...] = jnp.zeros_like(total)

    for row in range(row_block):
        entry = (step * row_block + row) * per_row
        products = [
            lax.dot_general(
                near[pos_ref[entry + k]],
                a_ref[row, k],
                (((1,), (1,)), ((), ())),
                preferred_element_type=jnp.float32,
            ).astype(jnp.bfloat16)
            for k in range(per_row)
        ]
        terms = jnp.dot(
            jnp.concatenate(products, axis=0), p_ref[row], preferred_element_type=jnp.float32
        )
        slots = [dst_ref[entry + k] for k in range(per_row)]
        sums = [
            total[slots[k]] + terms[k * height : (k + 1) * height] for k in range(per_row)
        ]
        for k in range(per_row):
            total[slots[k]] = sums[k]

    @pl.when(step == pl.num_programs(0) - 1)
    def _():
        half = keep_ref.shape[0]
        keep_ref[...] = total[:half].astype(keep_ref.dtype)
        send_ref[...] = total[half:].astype(send_ref.dtype)


def partial_sums(pos, dst, a_vals, p_vals, parts, slots):
    rows, per_row, side, _ = a_vals.shape
    height = parts[0].shape[1]
    half = slots // 2
    whole = lambda i, *_: (0, 0, 0)
    return pl.pallas_call(
        partial_kernel,
        grid_spec=pltpu.PrefetchScalarGridSpec(
            num_scalar_prefetch=2,
            grid=(rows // ROW_BLOCK,),
            in_specs=[
                pl.BlockSpec((ROW_BLOCK, per_row, side, side), lambda i, *_: (i, 0, 0, 0)),
                pl.BlockSpec((ROW_BLOCK, side, side), lambda i, *_: (i, 0, 0)),
            ]
            + [pl.BlockSpec((rows, height, side), whole)] * len(parts),
            out_specs=[pl.BlockSpec((half, height, side), whole)] * 2,
            scratch_shapes=[
                pltpu.VMEM((len(parts) * rows, height, side), jnp.bfloat16),
                pltpu.VMEM((slots, height, side), jnp.float32),
            ],
        ),
        out_shape=[jax.ShapeDtypeStruct((half, height, side), jnp.bfloat16)] * 2,
        compiler_params=pltpu.CompilerParams(vmem_limit_bytes=VMEM_BYTES),
        cost_estimate=pl.CostEstimate(
            flops=4 * rows * per_row * height * side * side,
            bytes_accessed=2 * a_vals.size + 2 * p_vals.size + 4 * slots * height * side,
            transcendentals=0,
        ),
        name="partial",
    )(pos, dst, a_vals, p_vals, *parts)


def finish_kernel(*refs):
    *pairs, out_ref = refs
    for slot in range(out_ref.shape[0]):
        sums = [
            pairs[j][slot].astype(jnp.float32) + pairs[j + 1][slot].astype(jnp.float32)
            for j in range(0, len(pairs), 2)
        ]
        out_ref[slot] = jnp.concatenate(sums, axis=0).T


def finish(pairs):
    slots, _, side = pairs[0][0].shape
    block = 8
    flat = [array for pair in pairs for array in pair]
    return pl.pallas_call(
        finish_kernel,
        grid=(slots // block,),
        in_specs=[
            pl.BlockSpec((block, array.shape[1], side), lambda i: (i, 0, 0)) for array in flat
        ],
        out_specs=pl.BlockSpec((block, side, side), lambda i: (i, 0, 0)),
        out_shape=jax.ShapeDtypeStruct((slots, side, side), jnp.float32),
        name="finish",
    )(*flat)


def gather_planes(own, planes):
    got = {0: own}
    if planes == 4:
        got[1] = lax.ppermute(own, "grp", flip(planes, 1))
        got[3] = lax.ppermute(own, "grp", flip(planes, 3))
        got[2] = lax.ppermute(got[3], "grp", flip(planes, 1))
    else:
        for bit in range(1, planes):
            got[bit] = lax.ppermute(own, "grp", flip(planes, bit))
    return [got[plane] for plane in range(planes)]


def halve(array, bits):
    owners = lax.axis_size("wide")
    keep, send = array
    for at, bit in enumerate(bits):
        got = lax.ppermute(send, "wide", flip(owners, bit))
        if at == len(bits) - 1:
            return keep, got
        half = keep.shape[0] // 2
        send = keep[half:] + got[half:]
        keep = keep[:half] + got[:half]


def on_device(slot_count, heights, a_vals, a_cols, p_vals, tile_slot):
    rows = a_vals.shape[0]
    owners, planes = lax.axis_size("wide"), lax.axis_size("grp")
    me, plane = lax.axis_index("wide"), lax.axis_index("grp")
    pos = ((a_cols // (owners * rows)) ^ plane) * rows + a_cols % rows
    relative = (tile_slot // slot_count % owners) ^ me
    bit_count = owners.bit_length() - 1
    orders = [list(range(bit_count))]
    orders.append([0] + orders[0][:0:-1])

    def place(order):
        spot = jnp.zeros_like(relative)
        for bit in order:
            spot = spot * 2 + (relative >> bit) % 2
        return (spot * slot_count + tile_slot % slot_count).reshape(-1)

    places = [place(order) for order in orders]
    pos = pos.reshape(-1)
    chunks = transposed_chunks(p_vals, heights)
    pairs = []
    for j, chunk in enumerate(chunks):
        parts = gather_planes(chunk, planes)
        send, keep = partial_sums(
            pos, places[j % 2], a_vals, p_vals, parts, owners * slot_count
        )
        pairs.append(halve((keep, send), [1 << bit for bit in orders[j % 2]]))
    return finish(pairs)


def solution(mesh):
    owners = mesh.shape["wide"]
    heights = (32, 32, 32, 32)
    placed = (
        P(("grp", "wide"), None, None, None),
        P(("grp", "wide"), None),
        P(("grp", "wide"), None, None),
        P(("grp", "wide"), None),
    )
    return jax.shard_map(
        functools.partial(on_device, 64, heights),
        mesh=mesh,
        in_specs=placed,
        out_specs=P(("grp", "wide"), None, None),
        check_vma=False,
    )
```

```python
import jax
import jax.numpy as jnp
from jax import lax
from jax.experimental import pallas as pl
from jax.experimental.pallas import tpu as pltpu
from jax.sharding import PartitionSpec as P

SLOT_DEV = 64
MIB = 2**20
VMEM = pl.BlockSpec(memory_space=pltpu.VMEM)
SMEM = pl.BlockSpec(memory_space=pltpu.SMEM)


def flip(size, bit):
    return [(i, i ^ bit) for i in range(size)]


def unit(side):
    shape = (side, side)
    same = lax.broadcasted_iota(jnp.int32, shape, 0) == lax.broadcasted_iota(jnp.int32, shape, 1)
    return same.astype(jnp.bfloat16)


def across(left, right, axes):
    return lax.dot_general(
        left, right, (((axes[0],), (axes[1],)), ((), ())), preferred_element_type=jnp.float32
    )


def turn_kernel(p_ref, *chunk_refs):
    eye = unit(p_ref.shape[1])
    for row in range(p_ref.shape[0]):
        turned = across(eye, p_ref[row], (1, 1)).astype(jnp.bfloat16)
        first = 0
        for chunk in chunk_refs:
            chunk[row] = turned[first : first + chunk.shape[1]]
            first += chunk.shape[1]


def turned_chunks(p_vals, heights):
    rows, side, _ = p_vals.shape
    block = rows // 2
    return pl.pallas_call(
        turn_kernel,
        grid=(rows // block,),
        in_specs=[pl.BlockSpec((block, side, side), lambda i: (i, 0, 0))],
        out_specs=[pl.BlockSpec((block, h, side), lambda i: (i, 0, 0)) for h in heights],
        out_shape=[jax.ShapeDtypeStruct((rows, h, side), p_vals.dtype) for h in heights],
        compiler_params=pltpu.CompilerParams(vmem_limit_bytes=8 * MIB),
        name="turn",
    )(p_vals)


def factor_kernel(a_ref, p_ref, factor_ref):
    block, per_row = a_ref.shape[0], a_ref.shape[1]
    first = pl.program_id(0) * block
    for row in range(block):
        for k in range(per_row):
            factor_ref[first + row, k] = across(a_ref[row, k], p_ref[row], (0, 0)).astype(
                jnp.bfloat16
            )


def factors(a_vals, p_vals):
    rows, per_row, side, _ = a_vals.shape
    block = 8
    return pl.pallas_call(
        factor_kernel,
        grid=(rows // block,),
        in_specs=[
            pl.BlockSpec((block, per_row, side, side), lambda i: (i, 0, 0, 0)),
            pl.BlockSpec((block, side, side), lambda i: (i, 0, 0)),
        ],
        out_specs=VMEM,
        out_shape=jax.ShapeDtypeStruct(a_vals.shape, jnp.bfloat16),
        compiler_params=pltpu.CompilerParams(vmem_limit_bytes=20 * MIB),
        cost_estimate=pl.CostEstimate(
            flops=2 * a_vals.size * side, bytes_accessed=4 * a_vals.size, transcendentals=0
        ),
        name="factors",
    )(a_vals, p_vals)


def partial_kernel(pos_ref, dst_ref, factor_ref, *refs):
    planes = len(refs) - 4
    parts = refs[:planes]
    send_ref, keep_ref, near, total = refs[planes:]
    rows, per_row = factor_ref.shape[0], factor_ref.shape[1]
    block = 8
    total[...] = jnp.zeros_like(total)
    for plane, part in enumerate(parts):
        near[plane * rows : (plane + 1) * rows] = part[...]

    def some_rows(step, carry):
        for at in range(block):
            row = step * block + at
            terms = [
                jnp.dot(
                    near[pos_ref[k, row]],
                    factor_ref[row, k],
                    preferred_element_type=jnp.float32,
                )
                for k in range(per_row)
            ]
            slots = [dst_ref[k, row] for k in range(per_row)]
            sums = [total[slots[k]] + terms[k] for k in range(per_row)]
            for k in range(per_row):
                total[slots[k]] = sums[k]
        return carry

    lax.fori_loop(0, rows // block, some_rows, 0)
    half = keep_ref.shape[0]
    send_ref[...] = total[half:].astype(send_ref.dtype)
    keep_ref[...] = total[:half].astype(keep_ref.dtype)


def partial_sums(pos, dst, factor, parts, slots):
    rows, per_row, side, _ = factor.shape
    height = parts[0].shape[1]
    half = slots // 2
    return pl.pallas_call(
        partial_kernel,
        in_specs=[SMEM, SMEM, VMEM] + [VMEM] * len(parts),
        out_specs=[VMEM, VMEM],
        out_shape=[jax.ShapeDtypeStruct((half, height, side), jnp.bfloat16)] * 2,
        scratch_shapes=[
            pltpu.VMEM((len(parts) * rows, height, side), jnp.bfloat16),
            pltpu.VMEM((slots, height, side), jnp.float32),
        ],
        compiler_params=pltpu.CompilerParams(
            vmem_limit_bytes=4 * slots * height * side + 3 * MIB
        ),
        cost_estimate=pl.CostEstimate(
            flops=2 * rows * per_row * height * side * side,
            bytes_accessed=2 * factor.size + 2 * slots * height * side,
            transcendentals=0,
        ),
        name="partial",
    )(pos, dst, factor, *parts)


def finish_kernel(*refs):
    *pairs, out_ref = refs
    eye = unit(out_ref.shape[1])
    twice = jnp.concatenate([eye, eye], axis=1)
    for slot in range(out_ref.shape[0]):
        kept = jnp.concatenate([ref[slot] for ref in pairs[0::2]], axis=0)
        got = jnp.concatenate([ref[slot] for ref in pairs[1::2]], axis=0)
        out_ref[slot] = across(twice, jnp.concatenate([kept, got], axis=1), (1, 1))


def finish(pairs):
    slots, _, side = pairs[0][0].shape
    block = slots // 2
    flat = [array for pair in pairs for array in pair]
    return pl.pallas_call(
        finish_kernel,
        grid=(slots // block,),
        in_specs=[
            pl.BlockSpec((block, array.shape[1], side), lambda i: (i, 0, 0)) for array in flat
        ],
        out_specs=pl.BlockSpec((block, side, side), lambda i: (i, 0, 0)),
        out_shape=jax.ShapeDtypeStruct((slots, side, side), jnp.float32),
        compiler_params=pltpu.CompilerParams(vmem_limit_bytes=16 * MIB),
        name="finish",
    )(*flat)


def on_device(heights, orders, a_vals, a_cols, p_vals, tile_slot):
    rows = a_vals.shape[0]
    owners, planes = lax.axis_size("wide"), lax.axis_size("grp")
    me, plane = lax.axis_index("wide"), lax.axis_index("grp")
    columns, slots = a_cols.T, tile_slot.T
    pos = ((columns // (owners * rows)) ^ plane) * rows + columns % rows
    relative = (slots // SLOT_DEV % owners) ^ me
    places = []
    for order in orders:
        spot = jnp.zeros_like(relative)
        for bit in order:
            spot = spot * 2 + (relative >> bit) % 2
        places.append(spot * SLOT_DEV + slots % SLOT_DEV)
    chunks = turned_chunks(p_vals, heights)
    factor = factors(a_vals, p_vals)
    pairs = []
    for j, own in enumerate(chunks):
        got = {0: own}
        for bit in reversed(range(1, planes)):
            relay = planes == 4 and bit == 2
            got[bit] = lax.ppermute(
                got[3] if relay else own, "grp", flip(planes, 1 if relay else bit)
            )
        order = orders[j % len(orders)]
        send, keep = partial_sums(
            pos,
            places[j % len(orders)],
            factor,
            [got[bit] for bit in range(planes)],
            owners * SLOT_DEV,
        )
        for at, bit in enumerate(order):
            back = lax.ppermute(send, "wide", flip(owners, 1 << bit))
            if at == len(order) - 1:
                pairs.append((keep, back))
                break
            half = keep.shape[0] // 2
            send, keep = keep[half:] + back[half:], keep[:half] + back[:half]
    return finish(pairs)


def solution(mesh):
    owners = mesh.shape["wide"]
    moves = owners.bit_length() - 1
    height = max(16, min(32, 32 * 8 // owners))
    heights = (height,) * (128 // height)
    orders = [list(range(moves))]
    orders.append([0] + orders[0][:0:-1])
    placed = (
        P(("grp", "wide"), None, None, None),
        P(("grp", "wide"), None),
        P(("grp", "wide"), None, None),
        P(("grp", "wide"), None),
    )

    def program(*arrays):
        return on_device(heights, orders, *arrays)

    return jax.shard_map(
        program,
        mesh=mesh,
        in_specs=placed,
        out_specs=P(("grp", "wide"), None, None),
        check_vma=False,
    )
```

```python
import functools

import jax
import jax.numpy as jnp
from jax import lax
from jax.experimental import pallas as pl
from jax.experimental.pallas import tpu as pltpu
from jax.sharding import PartitionSpec as P

SLOT_DEV = 64
MIB = 2**20
HEIGHTS = (16, 32, 32, 32, 16)
VMEM = pl.BlockSpec(memory_space=pltpu.VMEM)
SMEM = pl.BlockSpec(memory_space=pltpu.SMEM)


def flip(size, bit):
    return [(i, i ^ bit) for i in range(size)]


def unit(side):
    shape = (side, side)
    same = lax.broadcasted_iota(jnp.int32, shape, 0) == lax.broadcasted_iota(jnp.int32, shape, 1)
    return same.astype(jnp.bfloat16)


def across(left, right, axes):
    return lax.dot_general(
        left, right, (((axes[0],), (axes[1],)), ((), ())), preferred_element_type=jnp.float32
    )


def turn_kernel(p_ref, *chunk_refs):
    eye = unit(p_ref.shape[1])
    for row in range(p_ref.shape[0]):
        turned = across(eye, p_ref[row], (1, 1)).astype(jnp.bfloat16)
        first = 0
        for chunk in chunk_refs:
            chunk[row] = turned[first : first + chunk.shape[1]]
            first += chunk.shape[1]


def turned_chunks(p_vals, heights):
    rows, side, _ = p_vals.shape
    block = rows // 2
    return pl.pallas_call(
        turn_kernel,
        grid=(rows // block,),
        in_specs=[pl.BlockSpec((block, side, side), lambda i: (i, 0, 0))],
        out_specs=[pl.BlockSpec((block, h, side), lambda i: (i, 0, 0)) for h in heights],
        out_shape=[jax.ShapeDtypeStruct((rows, h, side), p_vals.dtype) for h in heights],
        compiler_params=pltpu.CompilerParams(vmem_limit_bytes=8 * MIB),
        name="turn",
    )(p_vals)


def factor_kernel(a_ref, p_ref, factor_ref):
    block, per_row = a_ref.shape[0], a_ref.shape[1]
    first = pl.program_id(0) * block
    for row in range(block):
        for k in range(per_row):
            factor_ref[first + row, k] = across(a_ref[row, k], p_ref[row], (0, 0)).astype(
                jnp.bfloat16
            )


def factors(a_vals, p_vals):
    rows, per_row, side, _ = a_vals.shape
    block = 8
    return pl.pallas_call(
        factor_kernel,
        grid=(rows // block,),
        in_specs=[
            pl.BlockSpec((block, per_row, side, side), lambda i: (i, 0, 0, 0)),
            pl.BlockSpec((block, side, side), lambda i: (i, 0, 0)),
        ],
        out_specs=VMEM,
        out_shape=jax.ShapeDtypeStruct(a_vals.shape, jnp.bfloat16),
        compiler_params=pltpu.CompilerParams(vmem_limit_bytes=20 * MIB),
        cost_estimate=pl.CostEstimate(
            flops=2 * a_vals.size * side, bytes_accessed=4 * a_vals.size, transcendentals=0
        ),
        name="factors",
    )(a_vals, p_vals)


def partial_kernel(pos_ref, dst_ref, factor_ref, *refs):
    planes = len(refs) - 4
    parts = refs[:planes]
    send_ref, keep_ref, near, total = refs[planes:]
    rows, per_row = factor_ref.shape[0], factor_ref.shape[1]
    block = 8
    total[...] = jnp.zeros_like(total)
    for plane, part in enumerate(parts):
        near[plane * rows : (plane + 1) * rows] = part[...]

    def some_rows(step, carry):
        for at in range(block):
            row = step * block + at
            terms = [
                jnp.dot(
                    near[pos_ref[k, row]],
                    factor_ref[row, k],
                    preferred_element_type=jnp.float32,
                )
                for k in range(per_row)
            ]
            slots = [dst_ref[k, row] for k in range(per_row)]
            sums = [total[slots[k]] + terms[k] for k in range(per_row)]
            for k in range(per_row):
                total[slots[k]] = sums[k]
        return carry

    lax.fori_loop(0, rows // block, some_rows, 0)
    half = keep_ref.shape[0]
    send_ref[...] = total[half:].astype(send_ref.dtype)
    keep_ref[...] = total[:half].astype(keep_ref.dtype)


def partial_sums(pos, dst, factor, parts, slots):
    rows, per_row, side, _ = factor.shape
    height = parts[0].shape[1]
    half = slots // 2
    return pl.pallas_call(
        partial_kernel,
        in_specs=[SMEM, SMEM, VMEM] + [VMEM] * len(parts),
        out_specs=[VMEM, VMEM],
        out_shape=[jax.ShapeDtypeStruct((half, height, side), jnp.bfloat16)] * 2,
        scratch_shapes=[
            pltpu.VMEM((len(parts) * rows, height, side), jnp.bfloat16),
            pltpu.VMEM((slots, height, side), jnp.float32),
        ],
        compiler_params=pltpu.CompilerParams(
            vmem_limit_bytes=4 * slots * height * side + 3 * MIB
        ),
        cost_estimate=pl.CostEstimate(
            flops=2 * rows * per_row * height * side * side,
            bytes_accessed=2 * factor.size + 2 * slots * height * side,
            transcendentals=0,
        ),
        name="partial",
    )(pos, dst, factor, *parts)


def finish_kernel(streams, *refs):
    *arrays, out_ref = refs
    eye = unit(out_ref.shape[1])
    twice = jnp.concatenate([eye, eye], axis=1)
    for stream in range(streams):

        @pl.when(pl.program_id(0) == stream)
        def _(stream=stream):
            for slot in range(out_ref.shape[0]):
                kept = jnp.concatenate([ref[slot] for ref in arrays[2 * stream :: 2 * streams]], axis=0)
                got = jnp.concatenate([ref[slot] for ref in arrays[2 * stream + 1 :: 2 * streams]], axis=0)
                out_ref[slot] = across(twice, jnp.concatenate([kept, got], axis=1), (1, 1))


def finish(chunks):
    streams = len(chunks[0])
    block, _, side = chunks[0][0][0].shape
    flat = [array for chunk in chunks for pair in chunk for array in pair]
    return pl.pallas_call(
        functools.partial(finish_kernel, streams),
        grid=(streams,),
        in_specs=[VMEM] * len(flat),
        out_specs=pl.BlockSpec((block, side, side), lambda i: (i, 0, 0)),
        out_shape=jax.ShapeDtypeStruct((streams * block, side, side), jnp.float32),
        compiler_params=pltpu.CompilerParams(vmem_limit_bytes=16 * MIB),
        name="finish",
    )(*flat)


def on_device(heights, orders, a_vals, a_cols, p_vals, tile_slot):
    rows = a_vals.shape[0]
    owners, planes = lax.axis_size("wide"), lax.axis_size("grp")
    me, plane = lax.axis_index("wide"), lax.axis_index("grp")
    columns, slots = a_cols.T, tile_slot.T
    pos = ((columns // (owners * rows)) ^ plane) * rows + columns % rows
    relative = (slots // SLOT_DEV % owners) ^ me
    count = len(orders)
    each = SLOT_DEV // count
    local = slots % SLOT_DEV
    dst = jnp.zeros_like(slots)
    for stream, order in enumerate(orders):
        spot = jnp.zeros_like(relative)
        for bit in order[1:]:
            spot = spot * 2 + (relative >> bit) % 2
        spot = spot * each + local % each + stream * (owners // 2) * each
        dst = jnp.where(local // each == stream, spot, dst)
    dst = dst + (relative >> orders[0][0]) % 2 * (owners // 2) * SLOT_DEV
    chunks = turned_chunks(p_vals, heights)
    factor = factors(a_vals, p_vals)
    pairs = []
    for own in chunks:
        got = {0: own}
        for bit in reversed(range(1, planes)):
            relay = planes == 4 and bit == 2
            got[bit] = lax.ppermute(
                got[3] if relay else own, "grp", flip(planes, 1 if relay else bit)
            )
        send, keep = partial_sums(
            pos, dst, factor, [got[bit] for bit in range(planes)], owners * SLOT_DEV
        )
        back = lax.ppermute(send, "wide", flip(owners, 1 << orders[0][0]))
        pairs.append([])
        for stream, order in enumerate(orders):
            size = keep.shape[0] // count
            mine, theirs = (array[stream * size : (stream + 1) * size] for array in (keep, back))
            for bit in order[1:]:
                half = mine.shape[0] // 2
                out, mine = mine[half:] + theirs[half:], mine[:half] + theirs[:half]
                theirs = lax.ppermute(out, "wide", flip(owners, 1 << bit))
            pairs[-1].append((mine, theirs))
    return finish(pairs)


def solution(mesh):
    owners = mesh.shape["wide"]
    moves = owners.bit_length() - 1
    heights = HEIGHTS if owners <= 8 else (16,) * 8
    orders = [list(range(moves))]
    orders.append([0] + orders[0][:0:-1])
    placed = (
        P(("grp", "wide"), None, None, None),
        P(("grp", "wide"), None),
        P(("grp", "wide"), None, None),
        P(("grp", "wide"), None),
    )

    def program(*arrays):
        return on_device(heights, orders, *arrays)

    return jax.shard_map(
        program,
        mesh=mesh,
        in_specs=placed,
        out_specs=P(("grp", "wide"), None, None),
        check_vma=False,
    )
```

```python
import functools

import jax
import jax.numpy as jnp
from jax import lax
from jax.experimental import pallas as pl
from jax.experimental.pallas import tpu as pltpu
from jax.sharding import PartitionSpec as P

SLOT_DEV = 64
MIB = 2**20
HEIGHTS = (16, 32, 32, 32, 16)
VMEM = pl.BlockSpec(memory_space=pltpu.VMEM)
SMEM = pl.BlockSpec(memory_space=pltpu.SMEM)


def flip(size, bit):
    return [(i, i ^ bit) for i in range(size)]


def unit(side):
    shape = (side, side)
    same = lax.broadcasted_iota(jnp.int32, shape, 0) == lax.broadcasted_iota(jnp.int32, shape, 1)
    return same.astype(jnp.bfloat16)


def across(left, right, axes):
    return lax.dot_general(
        left, right, (((axes[0],), (axes[1],)), ((), ())), preferred_element_type=jnp.float32
    )


def turn_kernel(p_ref, *chunk_refs):
    eye = unit(p_ref.shape[1])
    for row in range(p_ref.shape[0]):
        turned = across(eye, p_ref[row], (1, 1)).astype(jnp.bfloat16)
        first = 0
        for chunk in chunk_refs:
            chunk[row] = turned[first : first + chunk.shape[1]]
            first += chunk.shape[1]


def turned_chunks(p_vals, heights):
    rows, side, _ = p_vals.shape
    block = rows // 2
    return pl.pallas_call(
        turn_kernel,
        grid=(rows // block,),
        in_specs=[pl.BlockSpec((block, side, side), lambda i: (i, 0, 0))],
        out_specs=[pl.BlockSpec((block, h, side), lambda i: (i, 0, 0)) for h in heights],
        out_shape=[jax.ShapeDtypeStruct((rows, h, side), p_vals.dtype) for h in heights],
        compiler_params=pltpu.CompilerParams(vmem_limit_bytes=8 * MIB),
        name="turn",
    )(p_vals)


def factor_kernel(a_ref, p_ref, factor_ref):
    block, per_row = a_ref.shape[0], a_ref.shape[1]
    first = pl.program_id(0) * block
    for row in range(block):
        for k in range(per_row):
            factor_ref[first + row, k] = across(a_ref[row, k], p_ref[row], (0, 0)).astype(
                jnp.bfloat16
            )


def factors(a_vals, p_vals):
    rows, per_row, side, _ = a_vals.shape
    block = 8
    return pl.pallas_call(
        factor_kernel,
        grid=(rows // block,),
        in_specs=[
            pl.BlockSpec((block, per_row, side, side), lambda i: (i, 0, 0, 0)),
            pl.BlockSpec((block, side, side), lambda i: (i, 0, 0)),
        ],
        out_specs=VMEM,
        out_shape=jax.ShapeDtypeStruct(a_vals.shape, jnp.bfloat16),
        compiler_params=pltpu.CompilerParams(vmem_limit_bytes=20 * MIB),
        cost_estimate=pl.CostEstimate(
            flops=2 * a_vals.size * side, bytes_accessed=4 * a_vals.size, transcendentals=0
        ),
        name="factors",
    )(a_vals, p_vals)


def partial_kernel(pos_ref, dst_ref, factor_ref, *refs):
    planes = len(refs) - 4
    parts = refs[:planes]
    send_ref, keep_ref, near, total = refs[planes:]
    rows, per_row = factor_ref.shape[0], factor_ref.shape[1]
    block = 8
    total[...] = jnp.zeros_like(total)
    for plane, part in enumerate(parts):
        near[plane * rows : (plane + 1) * rows] = part[...]

    def some_rows(step, carry):
        for at in range(block):
            row = step * block + at
            terms = [
                jnp.dot(
                    near[pos_ref[k, row]],
                    factor_ref[row, k],
                    preferred_element_type=jnp.float32,
                )
                for k in range(per_row)
            ]
            slots = [dst_ref[k, row] for k in range(per_row)]
            sums = [total[slots[k]] + terms[k] for k in range(per_row)]
            for k in range(per_row):
                total[slots[k]] = sums[k]
        return carry

    lax.fori_loop(0, rows // block, some_rows, 0)
    half = keep_ref.shape[0]
    send_ref[...] = total[half:].astype(send_ref.dtype)
    keep_ref[...] = total[:half].astype(keep_ref.dtype)


def partial_sums(pos, dst, factor, parts, slots):
    rows, per_row, side, _ = factor.shape
    height = parts[0].shape[1]
    half = slots // 2
    return pl.pallas_call(
        partial_kernel,
        in_specs=[SMEM, SMEM, VMEM] + [VMEM] * len(parts),
        out_specs=[VMEM, VMEM],
        out_shape=[jax.ShapeDtypeStruct((half, height, side), jnp.bfloat16)] * 2,
        scratch_shapes=[
            pltpu.VMEM((len(parts) * rows, height, side), jnp.bfloat16),
            pltpu.VMEM((slots, height, side), jnp.float32),
        ],
        compiler_params=pltpu.CompilerParams(
            vmem_limit_bytes=4 * slots * height * side + 3 * MIB
        ),
        cost_estimate=pl.CostEstimate(
            flops=2 * rows * per_row * height * side * side,
            bytes_accessed=2 * factor.size + 2 * slots * height * side,
            transcendentals=0,
        ),
        name="partial",
    )(pos, dst, factor, *parts)


def finish_kernel(streams, *refs):
    *arrays, out_ref = refs
    eye = unit(out_ref.shape[1])
    twice = jnp.concatenate([eye, eye], axis=1)
    block = out_ref.shape[0]
    splits = arrays[0].shape[0] // block
    for step in range(streams * splits):

        @pl.when(pl.program_id(0) == step)
        def _(stream=step // splits, first=step % splits * block):
            for at in range(block):
                slot = first + at
                kept = jnp.concatenate([ref[slot] for ref in arrays[2 * stream :: 2 * streams]], axis=0)
                got = jnp.concatenate([ref[slot] for ref in arrays[2 * stream + 1 :: 2 * streams]], axis=0)
                out_ref[at] = across(twice, jnp.concatenate([kept, got], axis=1), (1, 1))


def finish(chunks):
    streams = len(chunks[0])
    block, _, side = chunks[0][0][0].shape
    flat = [array for chunk in chunks for pair in chunk for array in pair]
    return pl.pallas_call(
        functools.partial(finish_kernel, streams),
        grid=(2 * streams,),
        in_specs=[VMEM] * len(flat),
        out_specs=pl.BlockSpec((block // 2, side, side), lambda i: (i, 0, 0)),
        out_shape=jax.ShapeDtypeStruct((streams * block, side, side), jnp.float32),
        compiler_params=pltpu.CompilerParams(vmem_limit_bytes=16 * MIB),
        name="finish",
    )(*flat)


def on_device(heights, orders, a_vals, a_cols, p_vals, tile_slot):
    rows = a_vals.shape[0]
    owners, planes = lax.axis_size("wide"), lax.axis_size("grp")
    me, plane = lax.axis_index("wide"), lax.axis_index("grp")
    columns, slots = a_cols.T, tile_slot.T
    pos = ((columns // (owners * rows)) ^ plane) * rows + columns % rows
    relative = (slots // SLOT_DEV % owners) ^ me
    count = len(orders)
    each = SLOT_DEV // count
    local = slots % SLOT_DEV
    dst = jnp.zeros_like(slots)
    for stream, order in enumerate(orders):
        spot = jnp.zeros_like(relative)
        for bit in order[1:]:
            spot = spot * 2 + (relative >> bit) % 2
        spot = spot * each + local % each + stream * (owners // 2) * each
        dst = jnp.where(local // each == stream, spot, dst)
    dst = dst + (relative >> orders[0][0]) % 2 * (owners // 2) * SLOT_DEV
    chunks = turned_chunks(p_vals, heights)
    factor = factors(a_vals, p_vals)
    pairs = []
    for own in chunks:
        got = {0: own}
        for bit in reversed(range(1, planes)):
            relay = planes == 4 and bit == 2
            got[bit] = lax.ppermute(
                got[3] if relay else own, "grp", flip(planes, 1 if relay else bit)
            )
        send, keep = partial_sums(
            pos, dst, factor, [got[bit] for bit in range(planes)], owners * SLOT_DEV
        )
        back = lax.ppermute(send, "wide", flip(owners, 1 << orders[0][0]))
        pairs.append([])
        for stream, order in enumerate(orders):
            size = keep.shape[0] // count
            mine, theirs = (array[stream * size : (stream + 1) * size] for array in (keep, back))
            for bit in order[1:]:
                half = mine.shape[0] // 2
                out, mine = mine[half:] + theirs[half:], mine[:half] + theirs[:half]
                theirs = lax.ppermute(out, "wide", flip(owners, 1 << bit))
            pairs[-1].append((mine, theirs))
    return finish(pairs)


def solution(mesh):
    owners = mesh.shape["wide"]
    moves = owners.bit_length() - 1
    heights = HEIGHTS if owners <= 8 else (16,) * 8
    orders = [list(range(moves))]
    orders.append([0] + orders[0][:0:-1])
    placed = (
        P(("grp", "wide"), None, None, None),
        P(("grp", "wide"), None),
        P(("grp", "wide"), None, None),
        P(("grp", "wide"), None),
    )

    def program(*arrays):
        return on_device(heights, orders, *arrays)

    return jax.shard_map(
        program,
        mesh=mesh,
        in_specs=placed,
        out_specs=P(("grp", "wide"), None, None),
        check_vma=False,
    )
```
